256 devices in a mesh: dp: 32 (over x, y, core), mp: 8 (over z).
Axes of the slice: x: 4, y: 4, z: 8, core: 2. Of those that a mesh axis runs over, the one named last changes fastest.
Arguments:
- weight: bfloat16 [1024, 128, 128], P(('dp', 'mp')), may hold values from -6 to 6
- moment_one: float32 [1024, 128, 128], P(('dp', 'mp')), may hold values from -1.8 to 1.8
- moment_two: float32 [1024, 128, 128], P(('dp', 'mp')), may hold values from 0.01 to 1
- block_row: int32 [1024], P(('dp', 'mp')), may hold values from 0 to 63, as said below
- block_col: int32 [1024], P(('dp', 'mp')), may hold values from 0 to 27
- dest_slot: int32 [1024], P(('dp', 'mp')), may hold values from -1 to 127, as said below
- tokens: bfloat16 [4096, 8192], P('dp', 'mp'), may hold values from -6 to 6
- upstream: bfloat16 [4096, 28672], P('dp', 'mp'), may hold values from -6 to 6
Outputs:
- new_weight: bfloat16 [1024, 128, 128], P(('dp', 'mp'))
- new_first: float32 [1024, 128, 128], P(('dp', 'mp'))
- new_second: float32 [1024, 128, 128], P(('dp', 'mp'))
- hidden_out: bfloat16 [4096, 28672], P('dp', 'mp')
- input_grad: bfloat16 [4096, 8192], P('dp', 'mp')
The draws below stay inside these ranges and needn't reach their ends.
Inputs may be any that keep to these rules, and one draw needn't show every extreme that they name: Within one tensor slice the pairs (block_row, block_col) are distinct. `dest_slot`: within one tensor slice the non-negative values are distinct; slots d * 4 to (d + 1) * 4 - 1 belong to dp index d, and a block held by dp index d goes to d - 1, d or d + 1; at most 2 blocks of one device go to each neighbour, and in every slice some pair of neighbours exchanges exactly 2 blocks each way.
All inputs are finite; a program needn't handle non-finite values.
Results may differ from the reference program's by a relative error of at most 0.0055.
Values may be sent and summed in bfloat16 or wider, within the bound.
A program may use at most 128 MiB of HBM per device.

```python
import math
import jax
import jax.numpy as jnp
from jax import lax

D = 8192
FF = 28672
BS = 128
KEPT_DEV = 4
TOKENS = 4096
KEPT = 128
SLICES = 8
KEPT_ALL = 1024
BLOCK_ROWS = 64
BLOCK_COLS = 28


def block_positions(key):
    slice_count = KEPT_ALL // KEPT
    column_count = FF // (BS * slice_count)
    positions_all = D // BS * column_count

    def one_slice(slice_index):
        slice_key = jax.random.fold_in(key, slice_index)
        first_key, second_key = jax.random.split(slice_key)
        inner_part = jax.random.permutation(first_key, positions_all - 2).astype(jnp.int32) + 1
        chosen = jnp.concatenate([jnp.array([0, positions_all - 1], dtype=jnp.int32), inner_part[:KEPT - 2]])
        return chosen[jax.random.permutation(second_key, KEPT)]
    position_list = jax.vmap(one_slice)(jnp.arange(slice_count, dtype=jnp.int32))
    position_list = jnp.swapaxes(position_list.reshape(slice_count, KEPT // KEPT_DEV, KEPT_DEV), 0, 1).reshape(KEPT_ALL)
    return (position_list, column_count)


def draw_block_row(key, part):
    position_list, column_count = block_positions(jax.random.fold_in(key, 101))
    return (position_list // column_count).astype(jnp.int32)


def draw_block_col(key, part):
    position_list, column_count = block_positions(jax.random.fold_in(key, 101))
    return (position_list % column_count).astype(jnp.int32)


def device_permutations(key, device_count):

    def permute_one(key_piece):
        return jax.random.permutation(key_piece, KEPT_DEV).astype(jnp.int32)
    return jax.vmap(permute_one)(jax.random.split(key, device_count))


def draw_dest_slot(key, part):
    slice_count = KEPT_ALL // KEPT
    device_count = KEPT // KEPT_DEV
    half_slots = KEPT_DEV // 2

    def one_slice(slice_index):
        base_key = jax.random.fold_in(jax.random.fold_in(key, 202), slice_index)
        key_list = jax.random.split(base_key, 5)
        crossing = jax.random.randint(key_list[0], (device_count,), 0, half_slots + 1).astype(jnp.int32)
        forced = jax.random.randint(key_list[1], (), 0, device_count - 1)
        device_ids = jnp.arange(device_count, dtype=jnp.int32)
        crossing = jnp.where(device_ids == forced, half_slots, crossing)
        crossing = jnp.where(device_ids == device_count - 1, 0, crossing)
        right_count = crossing[:, None]
        left_count = jnp.concatenate([jnp.zeros((1,), jnp.int32), crossing[:-1]])[:, None]
        ranking = device_permutations(key_list[2], device_count)
        going_left = ranking < left_count
        going_right = (ranking >= left_count) & (ranking < left_count + right_count)
        target = device_ids[:, None] + going_right.astype(jnp.int32) - going_left.astype(jnp.int32)
        item = jnp.where(going_left, KEPT_DEV - left_count + ranking, jnp.where(going_right, ranking - left_count, ranking - right_count))
        slot_order = device_permutations(key_list[3], device_count)
        new_slot = target * KEPT_DEV + slot_order[target, item]
        staying = jnp.logical_not(going_left | going_right)
        dropped = staying & (jax.random.randint(key_list[4], (device_count, KEPT_DEV), 0, 6) == 0) & (new_slot != KEPT - 1)
        forced_drop = staying & (device_ids[:, None] == 0) & (ranking == right_count)
        return jnp.where(dropped | forced_drop, -1, new_slot).astype(jnp.int32)
    slot_list = jax.vmap(one_slice)(jnp.arange(slice_count, dtype=jnp.int32))
    return jnp.swapaxes(slot_list, 0, 1).reshape(KEPT_ALL)


def shard_levels(stream_key, dims, cuts, least, high):
    level = 1.0
    for axis_at, parts in cuts:
        steps = jax.random.uniform(jax.random.fold_in(jax.random.fold_in(stream_key, 6), axis_at), (parts,), jnp.float32, least / len(cuts), high / len(cuts))
        level = level * jnp.repeat(jnp.exp(steps), dims[axis_at] // parts).reshape((-1,) + (1,) * (len(dims) - 1 - axis_at))
    return level


def normal_values(own_key, extent, scale, reach, shards=(), kind=jnp.bfloat16):
    values = jax.random.normal(own_key, extent, jnp.float32) * scale
    if len(shards) > 0:
        values = shard_levels(own_key, extent, shards, -0.22, 0.18) * values
    return jnp.clip(values, min=-reach, max=reach).astype(kind)


def setup_inputs(seed: int = 0) -> dict:
    seeds = jax.random.split(jax.random.key(seed), 9)
    return {
        "weight": normal_values(seeds[0], (KEPT_ALL, BS, BS), 1.0, 6.0, ((0, 256),)),
        "moment_one": normal_values(seeds[1], (KEPT_ALL, BS, BS), 0.3, 1.8, ((0, 256),), jnp.float32),
        "moment_two": jnp.clip(jnp.exp(math.log(1.0) - 4.6051702 * jax.random.uniform(seeds[2], (KEPT_ALL, BS, BS), jnp.float32) ** shard_levels(seeds[2], (KEPT_ALL, BS, BS), ((0, 256),), -0.2, 0.2)), 0.01, 1.0),
        "block_row": draw_block_row(jax.random.fold_in(seeds[8], 71), 0),
        "block_col": draw_block_col(jax.random.fold_in(seeds[8], 71), 0),
        "dest_slot": draw_dest_slot(jax.random.fold_in(seeds[8], 71), 0),
        "tokens": normal_values(seeds[6], (TOKENS, D), 1.0, 6.0, ((0, 32), (1, 8))),
        "upstream": normal_values(seeds[7], (TOKENS, FF), 1.0, 6.0, ((0, 32), (1, 8))),
    }


learn_rate = 0.02
beta_first = 0.9
beta_second = 0.95
epsilon = 1e-08
highest = lax.Precision.HIGHEST

def slice_view(array):
    rest_shape = array.shape[1:]
    grouped = array.reshape((KEPT // KEPT_DEV, SLICES, KEPT_DEV) + rest_shape)
    return jnp.swapaxes(grouped, 0, 1).reshape((SLICES, KEPT) + rest_shape)

def slice_unview(array):
    rest_shape = array.shape[2:]
    grouped = array.reshape((SLICES, KEPT // KEPT_DEV, KEPT_DEV) + rest_shape)
    return jnp.swapaxes(grouped, 0, 1).reshape((KEPT_ALL,) + rest_shape)

def reference(weight, moment_one, moment_two, block_row, block_col, dest_slot, tokens, upstream):
    grad_scale = 1.0 / math.sqrt(D)
    token_view = tokens.reshape(TOKENS, BLOCK_ROWS, BS)
    upstream_view = jnp.swapaxes(upstream.reshape(TOKENS, SLICES, BLOCK_COLS * BS), 0, 1)

    def one_slice(carry, pieces):
        slice_weight, slice_first, slice_second, slice_rows, slice_cols, slice_dest, slice_upstream = pieces
        x_blocks = jnp.take(token_view, slice_rows, axis=1).astype(jnp.float32)
        d_blocks = jnp.take(slice_upstream.reshape(TOKENS, BLOCK_COLS, BS), slice_cols, axis=1).astype(jnp.float32)
        w_float = slice_weight.astype(jnp.float32)
        forward = jnp.einsum('tbk,bkj->tbj', x_blocks, w_float, precision=highest)
        col_sums = jax.ops.segment_sum(jnp.swapaxes(forward, 0, 1), slice_cols, num_segments=BLOCK_COLS)
        hidden = (jnp.swapaxes(col_sums, 0, 1) * grad_scale).reshape(TOKENS, BLOCK_COLS * BS).astype(jnp.bfloat16)
        backward = jnp.einsum('tbj,bkj->tbk', d_blocks, w_float, precision=highest)
        row_sums = jax.ops.segment_sum(jnp.swapaxes(backward, 0, 1), slice_rows, num_segments=BLOCK_ROWS)
        partial_in = jnp.swapaxes(row_sums, 0, 1).reshape(TOKENS, D) * grad_scale
        gradient = jnp.einsum('tbk,tbj->bkj', x_blocks, d_blocks, precision=highest) * grad_scale
        first_new = beta_first * slice_first + (1.0 - beta_first) * gradient
        second_new = beta_second * slice_second + (1.0 - beta_second) * gradient * gradient
        stepped = (w_float - learn_rate * first_new / (jnp.sqrt(second_new) + epsilon)).astype(jnp.bfloat16)
        target_slot = jnp.where(slice_dest >= 0, slice_dest, KEPT).astype(jnp.int32)
        placed_weight = jnp.zeros((KEPT, BS, BS), jnp.bfloat16).at[target_slot].set(stepped, mode='drop')
        placed_first = jnp.zeros((KEPT, BS, BS), jnp.float32).at[target_slot].set(first_new, mode='drop')
        placed_second = jnp.zeros((KEPT, BS, BS), jnp.float32).at[target_slot].set(second_new, mode='drop')
        return (carry + partial_in, (hidden, placed_weight, placed_first, placed_second))
    pieces_all = (slice_view(weight), slice_view(moment_one), slice_view(moment_two), slice_view(block_row), slice_view(block_col), slice_view(dest_slot), upstream_view)
    input_sum, outputs = lax.scan(one_slice, jnp.zeros((TOKENS, D), jnp.float32), pieces_all)
    hidden_all, weight_all, first_all, second_all = outputs
    hidden_out = jnp.swapaxes(hidden_all, 0, 1).reshape(TOKENS, FF)
    return (slice_unview(weight_all), slice_unview(first_all), slice_unview(second_all), hidden_out, input_sum.astype(jnp.bfloat16))
```

```python
import math

import jax
import jax.numpy as jnp
from jax import lax
from jax.experimental import pallas as pl
from jax.experimental.pallas import tpu as pltpu
from jax.sharding import PartitionSpec as P

D = 8192
BS = 128
SCALE = 1.0 / math.sqrt(D)
LEARN = 0.02
B1 = 0.9
B2 = 0.95
EPS = 1e-08
NSEM = 128
MESH = pl.DeviceIdType.MESH

F32 = jnp.float32
BF16 = jnp.bfloat16
I32 = jnp.int32

UP = [(1, 0), (2, 1), (2, 0), (3, 1), (3, 0), (4, 1), (4, 0)]
DN = [(1, 1), (2, 0), (2, 1), (3, 0), (3, 1), (4, 0), (4, 1)]


def kernel(
    brow, bcol, bdst, weight, m1_in, m2_in, tokens, upstream,
    new_w, new_1, new_2, hidden, in_grad,
    x_all, w_all, meta, d_all, mom1, mom2, seg_b, seg_f, tab_v, tab,
    g_out, g_in, g_own, recv1, q_sum, recv2, zsend, zrecv,
    lsem, ssem, rsem,
):
    dp = lax.axis_index("dp")
    z = lax.axis_index("mp")
    c = lax.rem(dp, 2)
    y = lax.rem(dp // 2, 4)
    x = dp // 8

    def dev(xx, yy, cc, zz):
        return {"dp": (xx * 4 + yy) * 2 + cc, "mp": zz}

    def m4(v):
        return lax.rem(v + 8, 4)

    def m8(v):
        return lax.rem(v + 16, 8)

    zup, zdn = dev(x, y, c, m8(z + 1)), dev(x, y, c, m8(z - 1))
    partner = dev(x, y, 1 - c, z)
    left = {"dp": lax.rem(dp + 31, 32), "mp": z}
    right = {"dp": lax.rem(dp + 1, 32), "mp": z}
    xp, xm = dev(m4(x + 1), y, c, z), dev(m4(x - 1), y, c, z)
    yp, ym = dev(x, m4(y + 1), c, z), dev(x, m4(y - 1), c, z)

    def plus(h):
        return xp if h == 0 else yp

    def minus(h):
        return xm if h == 0 else ym

    counter = [0]
    pending = []

    def send(src, dst, device):
        i = counter[0]
        counter[0] += 1
        cp = pltpu.make_async_remote_copy(
            src_ref=src, dst_ref=dst, send_sem=ssem.at[i], recv_sem=rsem.at[i],
            device_id=device, device_id_type=MESH,
        )
        cp.start()
        pending.append(cp)
        return i, device

    def arrive(tag, region):
        i, device = tag
        pltpu.make_async_remote_copy(
            src_ref=region, dst_ref=region, send_sem=ssem.at[i], recv_sem=rsem.at[i],
            device_id=device, device_id_type=MESH,
        ).wait_recv()

    lcount = [0]

    def local(src, dst):
        i = lcount[0]
        lcount[0] += 1
        cp = pltpu.make_async_copy(src, dst, lsem.at[i])
        cp.start()
        return cp

    tok_cp = [local(tokens.at[:, pl.ds(i * BS, BS)], x_all.at[z * 8 + i]) for i in range(8)]
    w_cp = [local(weight.at[pl.ds(2 * h, 2)], w_all.at[x, y, c, h]) for h in range(2)]
    mom_cp = [local(m1_in, mom1.at[1]), local(m2_in, mom2.at[1])]
    d_cp = [local(upstream.at[:, pl.ds(i * BS, BS)], d_all.at[i]) for i in range(28)]

    sub8 = lax.broadcasted_iota(I32, (8, BS), 0)
    lane8 = lax.broadcasted_iota(I32, (8, BS), 1)
    own_meta = jnp.zeros((8, BS), I32)
    for j in range(4):
        at = lane8 == dp * 4 + j
        for r, ref in enumerate((brow, bcol, bdst)):
            own_meta = own_meta + jnp.where(at & (sub8 == r), ref[j], 0)
    meta[x, y, c] = own_meta

    off = {"dp": lax.rem(dp + 31 + 2 * c, 32), "mp": z}
    barrier = pltpu.get_barrier_semaphore()
    for peer in (zup, zdn, partner, off, xp, xm, yp, ym):
        pl.semaphore_signal(barrier, inc=1, device_id=peer, device_id_type=MESH)
    pl.semaphore_wait(barrier, 8)

    def xs(level, h):
        return x_all.at[pl.ds(level * 8 + h * 4, 4)]

    zt = {0: {}, 1: {}}

    def z_send(dirn, i):
        k, h = divmod(i, 2)
        if i == 6:
            h = dirn
        level = m8(z - k) if dirn == 0 else m8(z + k)
        zt[dirn][i] = send(xs(level, h), xs(level, h), zup if dirn == 0 else zdn)

    def z_wait(dirn, i):
        k, h = divmod(i, 2)
        if i == 6:
            h = dirn
        level = m8(z - k - 1) if dirn == 0 else m8(z + k + 1)
        arrive(zt[dirn][i], xs(level, h))

    def z_event(i):
        for dirn in (0, 1):
            z_wait(dirn, i)
            if i + 2 < 6:
                z_send(dirn, i + 2)
            elif i + 2 == 6 + dirn:
                z_send(dirn, 6)

    for cp in w_cp:
        cp.wait()
    mt = [send(meta.at[x, y, c], meta.at[x, y, c], d) for d in (xp, xm)]

    def w1(h, delta):
        return (m4(x + delta), y, c, h) if h == 0 else (x, m4(y + delta), c, h)

    w1t = {}
    for h in (0, 1):
        own = w_all.at[w1(h, 0)]
        w1t[h, 0] = send(own, own, plus(h))
        w1t[h, 1] = send(own, own, minus(h))
    for cp in tok_cp:
        cp.wait()
    for i in (0, 1):
        z_send(0, i)
        z_send(1, i)

    arrive(mt[0], meta.at[m4(x - 1), y, c])
    mt2 = send(meta.at[m4(x - 1), y, c], meta.at[m4(x - 1), y, c], xp)
    arrive(mt[1], meta.at[m4(x + 1), y, c])

    w1f = {}
    for h in (0, 1):
        arrive(w1t[h, 0], w_all.at[w1(h, -1)])
        r = w_all.at[w1(h, -1) + (0,)]
        w1f[h, 0] = send(r, r, plus(h))
        arrive(w1t[h, 1], w_all.at[w1(h, 1)])
        r = w_all.at[w1(h, 1) + (1,)]
        w1f[h, 1] = send(r, r, minus(h))
    arrive(mt2, meta.at[m4(x - 2), y, c])
    mt3 = [send(meta.at[:, y, c], meta.at[:, y, c], d) for d in (yp, ym)]
    z_event(0)
    for h in (0, 1):
        arrive(w1f[h, 0], w_all.at[w1(h, -2) + (0,)])
        arrive(w1f[h, 1], w_all.at[w1(h, 2) + (1,)])

    def w2(h, delta, cc):
        if h == 0:
            return (slice(None), m4(y + delta), cc, 0)
        return (m4(x + delta), slice(None), cc, 1)

    w2t = {}
    wpt = {}
    for h in (0, 1):
        own = w_all.at[w2(h, 0, c)]
        w2t[h, 0] = send(own, own, plus(1 - h))
        w2t[h, 1] = send(own, own, minus(1 - h))
    for h in (0, 1):
        own = w_all.at[w2(h, 0, c)]
        wpt[h, 0] = send(own, own, partner)
    arrive(mt3[0], meta.at[:, m4(y - 1), c])
    mt4 = send(meta.at[:, m4(y - 1), c], meta.at[:, m4(y - 1), c], yp)
    arrive(mt3[1], meta.at[:, m4(y + 1), c])
    z_event(1)
    arrive(mt4, meta.at[:, m4(y - 2), c])
    mt5 = send(meta.at[:, :, c], meta.at[:, :, c], partner)

    for cp in mom_cp:
        cp.wait()
    mom_t = []
    for ref in (mom1, mom2):
        mom_t.append((send(ref.at[1], ref.at[0], right), ref.at[0]))
        mom_t.append((send(ref.at[1], ref.at[2], left), ref.at[2]))
    arrive(mt5, meta.at[:, :, 1 - c])

    info = jnp.zeros((8, BS), I32)
    for a in range(4):
        for b in range(4):
            for cc in range(2):
                info = info + meta[a, b, cc]
    info = info.astype(F32)
    sub = lax.broadcasted_iota(I32, (BS, BS), 0)
    lane = lax.broadcasted_iota(I32, (BS, BS), 1)
    subf = sub.astype(F32)
    lanef = lane.astype(F32)

    def upright(v):
        return jnp.sum(
            jnp.where(sub == lane, jnp.broadcast_to(v, (BS, BS)), 0.0), axis=1, keepdims=True
        )

    def total(v):
        return jnp.sum(v, axis=0, keepdims=True)

    def ones(mask):
        return jnp.where(mask, 1.0, 0.0)

    row, col, dst = info[0:1], info[1:2], info[2:3]
    row_t, col_t, dst_t = upright(row), upright(col), upright(dst)

    def order(major, minor, major_t, minor_t, span):
        key, key_t = major * span + minor, major_t * span + minor_t
        pos_t = jnp.sum(ones(key < key_t), axis=1, keepdims=True)
        hot = ones(pos_t == lanef)
        who = total(subf * hot)
        major_s = total(major_t * hot)
        minor_s = total(minor_t * hot)
        start = total(ones(major_t < major_s))
        keep = jnp.where(start == lanef[0:1], 0.0, 1.0)
        upto = total(ones(major_t <= lanef))
        has = upto - total(ones(major_t < lanef))
        return who, minor_s, keep, jnp.maximum(upto - 1.0, 0.0), jnp.minimum(has, 1.0)

    rows = list(order(col, row, col_t, row_t, 64.0))
    rows += list(order(row, col, row_t, col_t, 32.0))
    hot = ones(dst_t == lanef)
    rows += [total(subf * hot), total(row_t * hot), total(col_t * hot), total(hot)]
    top = [127, 63, 1, 127, 1, 127, 27, 1, 127, 1, 127, 63, 27, 1]
    for i, v in enumerate(rows):
        tab_v[i : i + 1, :] = jnp.clip(v.astype(I32), 0, top[i])
    tab_cp = local(tab_v, tab)

    z_event(2)
    for h in (0, 1):
        arrive(w2t[h, 0], w_all.at[w2(h, -1, c)])
        r = w_all.at[w2(h, -1, c) + (0,)]
        w2t[h, 2] = send(r, r, plus(1 - h))
        arrive(w2t[h, 1], w_all.at[w2(h, 1, c)])
        r = w_all.at[w2(h, 1, c) + (1,)]
        w2t[h, 3] = send(r, r, minus(1 - h))
        for i, delta in ((1, -1), (2, 1)):
            r = w_all.at[w2(h, delta, c)]
            wpt[h, i] = send(r, r, partner)
    z_event(3)
    z_event(4)
    for h in (0, 1):
        arrive(w2t[h, 2], w_all.at[w2(h, -2, c) + (0,)])
        arrive(w2t[h, 3], w_all.at[w2(h, 2, c) + (1,)])
        r = w_all.at[w2(h, 2, c)]
        wpt[h, 3] = send(r, r, partner)
    z_event(5)
    for h in (0, 1):
        for i, delta in ((0, 0), (1, -1), (2, 1), (3, 2)):
            arrive(wpt[h, i], w_all.at[w2(h, delta, 1 - c)])
    for cp in d_cp:
        cp.wait()
    tab_cp.wait()

    def wblock(s):
        return w_all[s // 32, lax.rem(s // 8, 4), lax.rem(s // 4, 2), lax.rem(s // 2, 2), lax.rem(s, 2)]

    def bwd(p, acc):
        prod = lax.dot_general(
            d_all[tab[6, p]], wblock(tab[5, p]), (((1,), (1,)), ((), ())),
            preferred_element_type=F32,
        )
        acc = acc * tab[7, p].astype(F32) + prod
        seg_b[p] = acc
        return acc

    lax.fori_loop(0, BS, bwd, jnp.zeros((BS, BS), F32), unroll=4)

    def own_part(r):
        return seg_b[tab[8, r]] * (tab[9, r].astype(F32) * SCALE)

    zr = {0: {}, 1: {}}

    def zr_send(dirn, i):
        k, h = (UP, DN)[dirn][i]
        level = m8(z + 5 - k) if dirn == 0 else m8(z - 5 + k)
        if i >= 2:
            arrive(zr[dirn][i - 2], zrecv.at[dirn, i - 2])

        def one(b, carry):
            v = own_part(level * 8 + h * 4 + b)
            if i >= 2:
                v = v + zrecv[dirn, i - 2, b].astype(F32)
            zsend[dirn, i, b] = v.astype(BF16)
            return carry

        lax.fori_loop(0, 4, one, 0, unroll=True)
        zr[dirn][i] = send(zsend.at[dirn, i], zrecv.at[dirn, i], zup if dirn == 0 else zdn)

    def zr_event(i):
        zr_send(0, i)
        zr_send(1, i)

    z_event_last = [zt[d][6] for d in (0, 1)]
    zr_event(0)
    zr_event(1)
    z_wait(0, 6)
    z_wait(1, 6)

    def grad(q):
        g = lax.dot_general(
            x_all[tab[11, q]], d_all[tab[12, q]], (((0,), (0,)), ((), ())),
            preferred_element_type=F32,
        )
        return g * (tab[13, q].astype(F32) * SCALE)

    gt = {}
    for a in range(4):
        def part(i, carry):
            b, k = i // 4, lax.rem(i, 4)
            q = ((a * 4 + b) * 2 + (1 - c)) * 4 + k
            g_out[a, b, k // 2, lax.rem(k, 2)] = grad(q).astype(BF16)
            return carry

        lax.fori_loop(0, 16, part, 0, unroll=4)
        gt[a] = send(g_out.at[a], g_in.at[a], partner)
        if a == 1:
            zr_event(2)
    for a in range(4):
        arrive(gt[a], g_in.at[a])

        def part(i, carry):
            b, k = i // 4, lax.rem(i, 4)
            q = ((a * 4 + b) * 2 + c) * 4 + k
            h, j = k // 2, lax.rem(k, 2)
            g_own[a, b, h, j] = (grad(q) + g_in[a, b, h, j].astype(F32)).astype(BF16)
            return carry

        lax.fori_loop(0, 16, part, 0, unroll=4)
        if a == 1:
            zr_event(3)

    def g1(h, delta, j):
        if h == 0:
            return (m4(x + delta), slice(None), 0, j)
        return (slice(None), m4(y + delta), 1, j)

    rt = {}
    for h in (0, 1):
        rt[h, 0, 0] = send(g_own.at[g1(h, 2, 0)], recv1.at[h, 0, 0], plus(h))
        rt[h, 1, 0] = send(g_own.at[g1(h, 2, 1)], recv1.at[h, 1, 0], minus(h))
    for h in (0, 1):
        rt[h, 0, 1] = send(g_own.at[g1(h, 1, 1)], recv1.at[h, 0, 1], plus(h))
        rt[h, 1, 1] = send(g_own.at[g1(h, -1, 0)], recv1.at[h, 1, 1], minus(h))

    def fwd(p, acc):
        prod = jnp.dot(x_all[tab[1, p]], wblock(tab[0, p]), preferred_element_type=F32)
        acc = acc * tab[2, p].astype(F32) + prod
        seg_f[p] = acc
        return acc

    acc = lax.fori_loop(0, 32, fwd, jnp.zeros((BS, BS), F32), unroll=4)
    zr_event(4)

    def g1_add(h, dirn):
        delta, j = (1, 0) if dirn == 0 else (-1, 1)
        arrive(rt[h, dirn, 0], recv1.at[h, dirn, 0])
        at = g1(h, delta, j)
        g_own[at] = (g_own[at].astype(F32) + recv1[h, dirn, 0].astype(F32)).astype(BF16)
        rt[h, dirn, 2] = send(
            g_own.at[at], recv1.at[h, dirn, 2], plus(h) if dirn == 0 else minus(h)
        )

    for h in (0, 1):
        g1_add(h, 0)
        g1_add(h, 1)
    acc = lax.fori_loop(32, 64, fwd, acc, unroll=4)
    zr_event(5)
    acc = lax.fori_loop(64, 96, fwd, acc, unroll=4)
    zr_event(6)

    for h in (0, 1):
        for dirn in (0, 1):
            arrive(rt[h, dirn, 1], recv1.at[h, dirn, 1])
            arrive(rt[h, dirn, 2], recv1.at[h, dirn, 2])
        for j in (0, 1):
            lo, hi = (2, 1) if j == 0 else (1, 2)
            q_sum[h, :, j] = (
                g_own[g1(h, 0, j)].astype(F32)
                + recv1[h, 0, lo].astype(F32)
                + recv1[h, 1, hi].astype(F32)
            ).astype(BF16)

    def pos2(h, delta):
        return m4(y + delta) if h == 0 else m4(x + delta)

    st = {}
    for h in (0, 1):
        st[h, 0, 0] = send(q_sum.at[h, pos2(h, 2), 0], recv2.at[h, 0, 0], plus(1 - h))
        st[h, 1, 0] = send(q_sum.at[h, pos2(h, 2), 1], recv2.at[h, 1, 0], minus(1 - h))
        st[h, 0, 1] = send(q_sum.at[h, pos2(h, 1), 1], recv2.at[h, 0, 1], plus(1 - h))
        st[h, 1, 1] = send(q_sum.at[h, pos2(h, -1), 0], recv2.at[h, 1, 1], minus(1 - h))
    acc = lax.fori_loop(96, 112, fwd, acc, unroll=4)
    for h in (0, 1):
        for dirn in (0, 1):
            delta, j = (1, 0) if dirn == 0 else (-1, 1)
            arrive(st[h, dirn, 0], recv2.at[h, dirn, 0])
            at = (h, pos2(h, delta), j)
            q_sum[at] = (q_sum[at].astype(F32) + recv2[h, dirn, 0].astype(F32)).astype(BF16)
            st[h, dirn, 2] = send(
                q_sum.at[at], recv2.at[h, dirn, 2], plus(1 - h) if dirn == 0 else minus(1 - h)
            )
    acc = lax.fori_loop(112, 128, fwd, acc, unroll=4)

    for i in range(28):
        v = seg_f[tab[3, i]] * (tab[4, i].astype(F32) * SCALE)
        hidden[:, i * BS : (i + 1) * BS] = v.astype(BF16)

    for dirn in (0, 1):
        arrive(zr[dirn][5], zrecv.at[dirn, 5])
        arrive(zr[dirn][6], zrecv.at[dirn, 6])
    for b in range(8):
        h, k = divmod(b, 4)
        v = own_part(z * 8 + b)
        v = v + zrecv[0, 5 if h == 1 else 6, k].astype(F32)
        v = v + zrecv[1, 5 if h == 0 else 6, k].astype(F32)
        in_grad[:, b * BS : (b + 1) * BS] = v.astype(BF16)

    for tag, region in mom_t:
        arrive(tag, region)
    for h in (0, 1):
        for dirn in (0, 1):
            arrive(st[h, dirn, 1], recv2.at[h, dirn, 1])
            arrive(st[h, dirn, 2], recv2.at[h, dirn, 2])
        for j in (0, 1):
            lo, hi = (2, 1) if j == 0 else (1, 2)
            g = (
                q_sum[h, pos2(h, 0), j].astype(F32)
                + recv2[h, 0, lo].astype(F32)
                + recv2[h, 1, hi].astype(F32)
            )
            q = dp * 4 + h * 2 + j
            s = tab[10, q]
            valid = tab[13, q].astype(F32)
            mi = jnp.clip(s - (dp - 1) * 4, 0, 11)
            first = B1 * mom1[mi // 4, lax.rem(mi, 4)] + (1.0 - B1) * g
            second = B2 * mom2[mi // 4, lax.rem(mi, 4)] + (1.0 - B2) * g * g
            stepped = wblock(s).astype(F32) - LEARN * first / (jnp.sqrt(second) + EPS)
            new_w[h * 2 + j] = (stepped * valid).astype(BF16)
            new_1[h * 2 + j] = first * valid
            new_2[h * 2 + j] = second * valid

    for cp in pending:
        cp.wait_send()


def body(weight, moment_one, moment_two, block_row, block_col, dest_slot, tokens, upstream):
    hbm = pl.BlockSpec(memory_space=pl.ANY)
    smem = pl.BlockSpec(memory_space=pltpu.SMEM)
    vmem = pl.BlockSpec(memory_space=pltpu.VMEM)
    return pl.pallas_call(
        kernel,
        name="step",
        out_shape=(
            jax.ShapeDtypeStruct((4, BS, BS), BF16),
            jax.ShapeDtypeStruct((4, BS, BS), F32),
            jax.ShapeDtypeStruct((4, BS, BS), F32),
            jax.ShapeDtypeStruct((128, 3584), BF16),
            jax.ShapeDtypeStruct((128, 1024), BF16),
        ),
        in_specs=[smem] * 3 + [hbm] * 5,
        out_specs=(vmem,) * 5,
        scratch_shapes=[
            pltpu.VMEM((64, BS, BS), BF16),
            pltpu.VMEM((4, 4, 2, 2, 2, BS, BS), BF16),
            pltpu.VMEM((4, 4, 2, 8, BS), I32),
            pltpu.VMEM((28, BS, BS), BF16),
            pltpu.VMEM((3, 4, BS, BS), F32),
            pltpu.VMEM((3, 4, BS, BS), F32),
            pltpu.VMEM((BS, BS, BS), F32),
            pltpu.VMEM((BS, BS, BS), F32),
            pltpu.VMEM((16, BS), I32),
            pltpu.SMEM((16, BS), I32),
            pltpu.VMEM((4, 4, 2, 2, BS, BS), BF16),
            pltpu.VMEM((4, 4, 2, 2, BS, BS), BF16),
            pltpu.VMEM((4, 4, 2, 2, BS, BS), BF16),
            pltpu.VMEM((2, 2, 3, 4, BS, BS), BF16),
            pltpu.VMEM((2, 4, 2, BS, BS), BF16),
            pltpu.VMEM((2, 2, 3, BS, BS), BF16),
            pltpu.VMEM((2, 7, 4, BS, BS), BF16),
            pltpu.VMEM((2, 7, 4, BS, BS), BF16),
            pltpu.SemaphoreType.DMA((48,)),
            pltpu.SemaphoreType.DMA((NSEM,)),
            pltpu.SemaphoreType.DMA((NSEM,)),
        ],
        compiler_params=pltpu.CompilerParams(
            collective_id=0, has_side_effects=True, vmem_limit_bytes=60 * 1024 * 1024
        ),
    )(block_row, block_col, dest_slot, weight, moment_one, moment_two, tokens, upstream)


def solution(mesh):
    return jax.shard_map(
        body,
        mesh=mesh,
        in_specs=(
            P(("dp", "mp"), None, None),
            P(("dp", "mp"), None, None),
            P(("dp", "mp"), None, None),
            P(("dp", "mp")),
            P(("dp", "mp")),
            P(("dp", "mp")),
            P("dp", "mp"),
            P("dp", "mp"),
        ),
        out_specs=(
            P(("dp", "mp"), None, None),
            P(("dp", "mp"), None, None),
            P(("dp", "mp"), None, None),
            P("dp", "mp"),
            P("dp", "mp"),
        ),
        check_vma=False,
    )
```

```python
import math

import jax
import jax.numpy as jnp
from jax import lax
from jax.experimental import pallas as pl
from jax.experimental.pallas import tpu as pltpu
from jax.sharding import PartitionSpec as P

D = 8192
BS = 128
SCALE = 1.0 / math.sqrt(D)
LEARN = 0.02
B1 = 0.9
B2 = 0.95
EPS = 1e-08
NSEM = 256
MESH = pl.DeviceIdType.MESH

F32 = jnp.float32
BF16 = jnp.bfloat16
I32 = jnp.int32

UP = [(1, 0), (1, 1)] + [(k, s) for k in (2, 3, 4) for s in (2, 3, 0, 1)]
DN = [(1, 2), (1, 3)] + [(k, s) for k in (2, 3, 4) for s in (0, 1, 2, 3)]
OFF = (2, 1, -1, 0)


def kernel(
    brow, bcol, bdst, weight, m1_in, m2_in, tokens, upstream,
    new_w, new_1, new_2, hidden, in_grad,
    x_all, w_all, meta, d_all, mom1, mom2, seg_b, seg_f, tab_v, tab,
    g_out, g_in, g_own, recv1, q_sum, recv2, zsend, zrecv,
    lsem, ssem, rsem,
):
    dp = lax.axis_index("dp")
    z = lax.axis_index("mp")
    c = lax.rem(dp, 2)
    y = lax.rem(dp // 2, 4)
    x = dp // 8

    def dev(xx, yy, cc, zz):
        return {"dp": (xx * 4 + yy) * 2 + cc, "mp": zz}

    def m4(v):
        return lax.rem(v + 8, 4)

    def m8(v):
        return lax.rem(v + 16, 8)

    zup, zdn = dev(x, y, c, m8(z + 1)), dev(x, y, c, m8(z - 1))
    partner = dev(x, y, 1 - c, z)
    left = {"dp": lax.rem(dp + 31, 32), "mp": z}
    right = {"dp": lax.rem(dp + 1, 32), "mp": z}
    x2, y2 = dev(m4(x + 2), y, c, z), dev(x, m4(y + 2), c, z)
    xp, xm = dev(m4(x + 1), y, c, z), dev(m4(x - 1), y, c, z)
    yp, ym = dev(x, m4(y + 1), c, z), dev(x, m4(y - 1), c, z)

    def plus(h):
        return xp if h == 0 else yp

    def minus(h):
        return xm if h == 0 else ym

    counter = [0]
    pending = []

    def send(src, dst, device):
        i = counter[0]
        counter[0] += 1
        cp = pltpu.make_async_remote_copy(
            src_ref=src, dst_ref=dst, send_sem=ssem.at[i], recv_sem=rsem.at[i],
            device_id=device, device_id_type=MESH,
        )
        cp.start()
        pending.append(cp)
        return i, device

    def arrive(tag, region):
        i, device = tag
        pltpu.make_async_remote_copy(
            src_ref=region, dst_ref=region, send_sem=ssem.at[i], recv_sem=rsem.at[i],
            device_id=device, device_id_type=MESH,
        ).wait_recv()

    lcount = [0]

    def local(src, dst):
        i = lcount[0]
        lcount[0] += 1
        cp = pltpu.make_async_copy(src, dst, lsem.at[i])
        cp.start()
        return cp

    tok_cp = [local(tokens.at[:, pl.ds(i * BS, BS)], x_all.at[z * 8 + i]) for i in range(8)]
    w_cp = local(weight, w_all.at[pl.ds(dp * 4, 4)])
    d_cp = [local(upstream.at[:, pl.ds(i * BS, BS)], d_all.at[i]) for i in range(28)]
    mom_cp = [local(m1_in, mom1.at[1]), local(m2_in, mom2.at[1])]

    sub8 = lax.broadcasted_iota(I32, (8, BS), 0)
    lane8 = lax.broadcasted_iota(I32, (8, BS), 1)
    own_meta = jnp.zeros((8, BS), I32)
    for j in range(4):
        at = lane8 == dp * 4 + j
        for r, ref in enumerate((brow, bcol, bdst)):
            own_meta = own_meta + jnp.where(at & (sub8 == r), ref[j], 0)
    meta[x, y, c] = own_meta

    off = {"dp": lax.rem(dp + 31 + 2 * c, 32), "mp": z}
    barrier = pltpu.get_barrier_semaphore()
    for peer in (zup, zdn, partner, off, xp, xm, yp, ym, x2, y2):
        pl.semaphore_signal(barrier, inc=1, device_id=peer, device_id_type=MESH)
    pl.semaphore_wait(barrier, 10)

    zt = {0: {}, 1: {}}

    def xs(level, s):
        return x_all.at[pl.ds(level * 8 + s * 2, 2)]

    def z_part(dirn, i):
        k, s = divmod(i, 4)
        return k, s + 2 * dirn if k == 3 else s

    def z_send(dirn, i):
        k, s = z_part(dirn, i)
        r = xs(m8(z - k) if dirn == 0 else m8(z + k), s)
        zt[dirn][i] = send(r, r, zup if dirn == 0 else zdn)

    def z_wait(dirn, i):
        k, s = z_part(dirn, i)
        arrive(zt[dirn][i], xs(m8(z - k - 1) if dirn == 0 else m8(z + k + 1), s))

    def z_event(i):
        for dirn in (0, 1):
            z_wait(dirn, i)
            if i + 4 < 12:
                z_send(dirn, i + 4)
            elif i < 12 and (i - 8) // 2 == dirn:
                z_send(dirn, 12 + i % 2)

    def wp(h, du, dv, cc, j=None):
        xx, yy = (m4(x + du), m4(y + dv)) if h == 0 else (m4(x + dv), m4(y + du))
        base = ((xx * 4 + yy) * 2 + cc) * 4 + h * 2
        return w_all.at[pl.ds(base, 2)] if j is None else w_all.at[pl.ds(base + j, 1)]

    wt = {}

    def w_send(key, r, device):
        wt[key] = send(r, r, device)

    def w_partner(h, du, dv):
        w_send(("p", h, du, dv), wp(h, du, dv, c), partner)

    def w_phase2(h, du):
        r = wp(h, du, 0, c)
        w_send((2, h, du, 0), r, plus(1 - h))
        w_send((2, h, du, 1), r, minus(1 - h))
        w_partner(h, du, 0)

    def w_turn(h, du):
        arrive(wt[2, h, du, 0], wp(h, du, -1, c))
        w_send((3, h, du, 0), wp(h, du, -1, c, 0), plus(1 - h))
        arrive(wt[2, h, du, 1], wp(h, du, 1, c))
        w_send((3, h, du, 1), wp(h, du, 1, c, 1), minus(1 - h))
        w_partner(h, du, -1)
        w_partner(h, du, 1)

    def w_last(h, du):
        arrive(wt[3, h, du, 0], wp(h, du, -2, c, 0))
        arrive(wt[3, h, du, 1], wp(h, du, 2, c, 1))
        w_partner(h, du, 2)

    for i in range(4):
        tok_cp[2 * i].wait()
        tok_cp[2 * i + 1].wait()
        z_send(0, i)
        z_send(1, i)
    mt = [send(meta.at[x, y, c], meta.at[x, y, c], d) for d in (xp, xm, x2)]
    w_cp.wait()
    for h in (0, 1):
        w_send((0, h, 0), wp(h, 0, 0, c), plus(h))
        w_send((0, h, 1), wp(h, 0, 0, c), minus(h))
    for h in (0, 1):
        w_phase2(h, 0)

    for tag, delta in zip(mt, (-1, 1, 2)):
        arrive(tag, meta.at[m4(x + delta), y, c])
    mt = [send(meta.at[:, y, c], meta.at[:, y, c], d) for d in (yp, ym, y2)]
    for h in (0, 1):
        arrive(wt[0, h, 0], wp(h, -1, 0, c))
        w_send((1, h, 0), wp(h, -1, 0, c, 0), plus(h))
        arrive(wt[0, h, 1], wp(h, 1, 0, c))
        w_send((1, h, 1), wp(h, 1, 0, c, 1), minus(h))
    for h in (0, 1):
        w_phase2(h, -1)
        w_phase2(h, 1)
    z_event(0)
    z_event(1)
    for h in (0, 1):
        w_turn(h, 0)
    z_event(2)
    for tag, delta in zip(mt, (-1, 1, 2)):
        arrive(tag, meta.at[:, m4(y + delta), c])
    mt = send(meta.at[:, :, c], meta.at[:, :, c], partner)
    for h in (0, 1):
        arrive(wt[1, h, 0], wp(h, -2, 0, c, 0))
        arrive(wt[1, h, 1], wp(h, 2, 0, c, 1))
        w_phase2(h, 2)
    z_event(3)
    arrive(mt, meta.at[:, :, 1 - c])

    info = jnp.zeros((8, BS), I32)
    for a in range(4):
        for b in range(4):
            for cc in range(2):
                info = info + meta[a, b, cc]
    info = info.astype(F32)
    sub = lax.broadcasted_iota(I32, (BS, BS), 0)
    lane = lax.broadcasted_iota(I32, (BS, BS), 1)
    subf = sub.astype(F32)
    lanef = lane.astype(F32)

    def upright(v):
        return jnp.sum(
            jnp.where(sub == lane, jnp.broadcast_to(v, (BS, BS)), 0.0), axis=1, keepdims=True
        )

    def total(v):
        return jnp.sum(v, axis=0, keepdims=True)

    def ones(mask):
        return jnp.where(mask, 1.0, 0.0)

    row, col, dst = info[0:1], info[1:2], info[2:3]
    row_t, col_t, dst_t = upright(row), upright(col), upright(dst)

    def order(major, minor, major_t, minor_t, span):
        key, key_t = major * span + minor, major_t * span + minor_t
        pos_t = jnp.sum(ones(key < key_t), axis=1, keepdims=True)
        hot = ones(pos_t == lanef)
        who = total(subf * hot)
        major_s = total(major_t * hot)
        minor_s = total(minor_t * hot)
        start = total(ones(major_t < major_s))
        keep = jnp.where(start == lanef[0:1], 0.0, 1.0)
        upto = total(ones(major_t <= lanef))
        has = upto - total(ones(major_t < lanef))
        return who, minor_s, keep, jnp.maximum(upto - 1.0, 0.0), jnp.minimum(has, 1.0)

    z_event(4)
    rows = list(order(col, row, col_t, row_t, 64.0))
    rows += list(order(row, col, row_t, col_t, 32.0))
    hot = ones(dst_t == lanef)
    rows += [total(subf * hot), total(row_t * hot), total(col_t * hot), total(hot)]
    top = [127, 63, 1, 127, 1, 127, 27, 1, 127, 1, 127, 63, 27, 1]
    for i, v in enumerate(rows):
        tab_v[i : i + 1, :] = jnp.clip(v.astype(I32), 0, top[i])
    tab_cp = local(tab_v, tab)

    z_event(5)
    for h in (0, 1):
        w_turn(h, -1)
        w_turn(h, 1)
    z_event(6)
    for h in (0, 1):
        w_last(h, 0)
        w_turn(h, 2)
    z_event(7)
    for h in (0, 1):
        w_last(h, -1)
        w_last(h, 1)
    z_event(8)
    for h in (0, 1):
        w_last(h, 2)
    z_event(9)

    for cp in mom_cp:
        cp.wait()
    mom_t = []
    for ref in (mom1, mom2):
        mom_t.append((send(ref.at[1], ref.at[0], right), ref.at[0]))
        mom_t.append((send(ref.at[1], ref.at[2], left), ref.at[2]))

    for h in (0, 1):
        for du in OFF:
            for dv in OFF:
                arrive(wt["p", h, du, dv], wp(h, du, dv, 1 - c))
    for cp in d_cp:
        cp.wait()
    tab_cp.wait()

    def run(start, stop, step, acc):
        def some(t, acc):
            for i in range(16):
                acc = step(start + t * 16 + i, acc)
            return acc

        return lax.fori_loop(0, (stop - start) // 16, some, acc)

    def bwd(p, acc):
        prod = lax.dot_general(
            d_all[tab[6, p]], w_all[tab[5, p]], (((1,), (1,)), ((), ())),
            preferred_element_type=F32,
        )
        acc = acc * tab[7, p].astype(F32) + prod
        seg_b[p] = acc
        return acc

    acc = run(0, 48, bwd, jnp.zeros((BS, BS), F32))
    z_event(10)
    acc = run(48, 96, bwd, acc)
    z_event(11)
    acc = run(96, 128, bwd, acc)

    def own_part(r):
        return seg_b[tab[8, r]] * (tab[9, r].astype(F32) * SCALE)

    zr = {0: {}, 1: {}}

    def zr_send(dirn, i):
        k, s = (UP, DN)[dirn][i]
        level = m8(z + 5 - k) if dirn == 0 else m8(z - 5 + k)
        if i >= 4:
            arrive(zr[dirn][i - 4], zrecv.at[dirn, i - 4])
        for b in range(2):
            v = own_part(level * 8 + s * 2 + b)
            if i >= 4:
                v = v + zrecv[dirn, i - 4, b].astype(F32)
            zsend[dirn, i, b] = v.astype(BF16)
        zr[dirn][i] = send(zsend.at[dirn, i], zrecv.at[dirn, i], zup if dirn == 0 else zdn)

    def zr_event(i):
        zr_send(0, i)
        zr_send(1, i)

    for i in range(4):
        zr_event(i)
    z_event(12)
    z_event(13)

    def grad(g, h, j, o, cc):
        u, v = OFF[g], OFF[o]
        xx, yy = (m4(x + u), m4(y + v)) if h == 0 else (m4(x + v), m4(y + u))
        q = ((xx * 4 + yy) * 2 + cc) * 4 + h * 2 + j
        r = lax.dot_general(
            x_all[tab[11, q]], d_all[tab[12, q]], (((0,), (0,)), ((), ())),
            preferred_element_type=F32,
        )
        return r * (tab[13, q].astype(F32) * SCALE)

    gt = {}
    members = [(h, j, o) for h in (0, 1) for j in (0, 1) for o in range(4)]
    for g in range(4):
        for h, j, o in members:
            g_out[g, h, j, o] = grad(g, h, j, o, 1 - c).astype(BF16)
        gt[g] = send(g_out.at[g], g_in.at[g], partner)

    def fwd(p, acc):
        prod = jnp.dot(x_all[tab[1, p]], w_all[tab[0, p]], preferred_element_type=F32)
        acc = acc * tab[2, p].astype(F32) + prod
        seg_f[p] = acc
        return acc

    facc = run(0, 32, fwd, jnp.zeros((BS, BS), F32))

    rt = {}

    def g1_send(key, src, device):
        h, dirn, n = key
        rt[key] = send(src, recv1.at[h, dirn, n], device)

    for g in range(4):
        arrive(gt[g], g_in.at[g])
        for h, j, o in members:
            v = grad(g, h, j, o, c) + g_in[g, h, j, o].astype(F32)
            g_own[g, h, j, o] = v.astype(BF16)
        for h in (0, 1):
            if g == 0:
                g1_send((h, 0, 0), g_own.at[0, h, 0], plus(h))
                g1_send((h, 1, 0), g_own.at[0, h, 1], minus(h))
            elif g == 1:
                g1_send((h, 0, 1), g_own.at[1, h, 1], plus(h))
            elif g == 2:
                g1_send((h, 1, 1), g_own.at[2, h, 0], minus(h))
        if g == 1:
            zr_event(4)
    zr_event(5)
    facc = run(32, 64, fwd, facc)
    zr_event(6)
    facc = run(64, 80, fwd, facc)
    zr_event(7)
    for h in (0, 1):
        for dirn in (0, 1):
            arrive(rt[h, dirn, 0], recv1.at[h, dirn, 0])
            at = (1, h, 0) if dirn == 0 else (2, h, 1)
            g_own[at] = (g_own[at].astype(F32) + recv1[h, dirn, 0].astype(F32)).astype(BF16)
            g1_send((h, dirn, 2), g_own.at[at], plus(h) if dirn == 0 else minus(h))
    zr_event(8)
    facc = run(80, 96, fwd, facc)
    zr_event(9)
    facc = run(96, 128, fwd, facc)
    zr_event(10)
    for i in range(28):
        v = seg_f[tab[3, i]] * (tab[4, i].astype(F32) * SCALE)
        hidden[:, i * BS : (i + 1) * BS] = v.astype(BF16)
    zr_event(11)

    st = {}

    def g2_send(key, src, device):
        h, dirn, n = key
        st[key] = send(src, recv2.at[h, dirn, n], device)

    for h in (0, 1):
        for dirn in (0, 1):
            arrive(rt[h, dirn, 1], recv1.at[h, dirn, 1])
            arrive(rt[h, dirn, 2], recv1.at[h, dirn, 2])
        for j in (0, 1):
            lo, hi = (2, 1) if j == 0 else (1, 2)
            q_sum[h, j] = (
                g_own[3, h, j].astype(F32)
                + recv1[h, 0, lo].astype(F32)
                + recv1[h, 1, hi].astype(F32)
            ).astype(BF16)
        g2_send((h, 0, 0), q_sum.at[h, 0, 0], plus(1 - h))
        g2_send((h, 1, 0), q_sum.at[h, 1, 0], minus(1 - h))
        g2_send((h, 0, 1), q_sum.at[h, 1, 1], plus(1 - h))
        g2_send((h, 1, 1), q_sum.at[h, 0, 2], minus(1 - h))
    zr_event(12)
    zr_event(13)
    for h in (0, 1):
        for dirn in (0, 1):
            arrive(st[h, dirn, 0], recv2.at[h, dirn, 0])
            at = (h, 0, 1) if dirn == 0 else (h, 1, 2)
            q_sum[at] = (q_sum[at].astype(F32) + recv2[h, dirn, 0].astype(F32)).astype(BF16)
            g2_send((h, dirn, 2), q_sum.at[at], plus(1 - h) if dirn == 0 else minus(1 - h))

    for s in (2, 3, 0, 1):
        iu, id_ = UP.index((4, s)), DN.index((4, s))
        arrive(zr[0][iu], zrecv.at[0, iu])
        arrive(zr[1][id_], zrecv.at[1, id_])
        for k in range(2):
            b = s * 2 + k
            v = own_part(z * 8 + b) + zrecv[0, iu, k].astype(F32) + zrecv[1, id_, k].astype(F32)
            in_grad[:, b * BS : (b + 1) * BS] = v.astype(BF16)

    for tag, region in mom_t:
        arrive(tag, region)
    for h in (0, 1):
        for dirn in (0, 1):
            arrive(st[h, dirn, 1], recv2.at[h, dirn, 1])
            arrive(st[h, dirn, 2], recv2.at[h, dirn, 2])
        for j in (0, 1):
            lo, hi = (2, 1) if j == 0 else (1, 2)
            g = (
                q_sum[h, j, 3].astype(F32)
                + recv2[h, 0, lo].astype(F32)
                + recv2[h, 1, hi].astype(F32)
            )
            q = dp * 4 + h * 2 + j
            s = tab[10, q]
            valid = tab[13, q].astype(F32)
            mi = jnp.clip(s - (dp - 1) * 4, 0, 11)
            first = B1 * mom1[mi // 4, lax.rem(mi, 4)] + (1.0 - B1) * g
            second = B2 * mom2[mi // 4, lax.rem(mi, 4)] + (1.0 - B2) * g * g
            stepped = w_all[s].astype(F32) - LEARN * first / (jnp.sqrt(second) + EPS)
            new_w[h * 2 + j] = (stepped * valid).astype(BF16)
            new_1[h * 2 + j] = first * valid
            new_2[h * 2 + j] = second * valid

    for cp in pending:
        cp.wait_send()


def store(a, b, c, d, e, oa, ob, oc, od, oe, sem):
    copies = [
        pltpu.make_async_copy(src, dst, sem.at[i])
        for i, (src, dst) in enumerate(((a, oa), (b, ob), (c, oc), (d, od), (e, oe)))
    ]
    for cp in copies:
        cp.start()
    for cp in copies:
        cp.wait()


def body(weight, moment_one, moment_two, block_row, block_col, dest_slot, tokens, upstream):
    hbm = pl.BlockSpec(memory_space=pl.ANY)
    smem = pl.BlockSpec(memory_space=pltpu.SMEM)
    vmem = pl.BlockSpec(memory_space=pltpu.VMEM)
    outs = (
        ((4, BS, BS), BF16), ((4, BS, BS), F32), ((4, BS, BS), F32),
        ((128, 3584), BF16), ((128, 1024), BF16),
    )
    made = pl.pallas_call(
        kernel,
        name="step",
        out_shape=tuple(pltpu.VMEM(s, t) for s, t in outs),
        in_specs=[smem] * 3 + [hbm] * 5,
        out_specs=(vmem,) * 5,
        scratch_shapes=[
            pltpu.VMEM((64, BS, BS), BF16),
            pltpu.VMEM((BS, BS, BS), BF16),
            pltpu.VMEM((4, 4, 2, 8, BS), I32),
            pltpu.VMEM((28, BS, BS), BF16),
            pltpu.VMEM((3, 4, BS, BS), F32),
            pltpu.VMEM((3, 4, BS, BS), F32),
            pltpu.VMEM((BS, BS, BS), F32),
            pltpu.VMEM((BS, BS, BS), F32),
            pltpu.VMEM((16, BS), I32),
            pltpu.SMEM((16, BS), I32),
            pltpu.VMEM((4, 2, 2, 4, BS, BS), BF16),
            pltpu.VMEM((4, 2, 2, 4, BS, BS), BF16),
            pltpu.VMEM((4, 2, 2, 4, BS, BS), BF16),
            pltpu.VMEM((2, 2, 3, 4, BS, BS), BF16),
            pltpu.VMEM((2, 2, 4, BS, BS), BF16),
            pltpu.VMEM((2, 2, 3, BS, BS), BF16),
            pltpu.VMEM((2, 14, 2, BS, BS), BF16),
            pltpu.VMEM((2, 14, 2, BS, BS), BF16),
            pltpu.SemaphoreType.DMA((48,)),
            pltpu.SemaphoreType.DMA((NSEM,)),
            pltpu.SemaphoreType.DMA((NSEM,)),
        ],
        compiler_params=pltpu.CompilerParams(
            collective_id=0, has_side_effects=True, vmem_limit_bytes=62 * 1024 * 1024
        ),
    )(block_row, block_col, dest_slot, weight, moment_one, moment_two, tokens, upstream)
    return pl.pallas_call(
        store,
        name="store",
        out_shape=tuple(jax.ShapeDtypeStruct(s, t) for s, t in outs),
        in_specs=[pl.BlockSpec(memory_space=pltpu.VMEM)] * 5,
        out_specs=(hbm,) * 5,
        scratch_shapes=[pltpu.SemaphoreType.DMA((5,))],
        compiler_params=pltpu.CompilerParams(vmem_limit_bytes=2 * 1024 * 1024),
    )(*made)


def solution(mesh):
    return jax.shard_map(
        body,
        mesh=mesh,
        in_specs=(
            P(("dp", "mp"), None, None),
            P(("dp", "mp"), None, None),
            P(("dp", "mp"), None, None),
            P(("dp", "mp")),
            P(("dp", "mp")),
            P(("dp", "mp")),
            P("dp", "mp"),
            P("dp", "mp"),
        ),
        out_specs=(
            P(("dp", "mp"), None, None),
            P(("dp", "mp"), None, None),
            P(("dp", "mp"), None, None),
            P("dp", "mp"),
            P("dp", "mp"),
        ),
        check_vma=False,
    )
```

```python
import math

import jax
import jax.numpy as jnp
from jax import lax
from jax.experimental import pallas as pl
from jax.experimental.pallas import tpu as pltpu
from jax.sharding import PartitionSpec as P

D = 8192
BS = 128
SCALE = 1.0 / math.sqrt(D)
LEARN = 0.02
B1 = 0.9
B2 = 0.95
EPS = 1e-08
NSEM = 256
MESH = pl.DeviceIdType.MESH

F32 = jnp.float32
BF16 = jnp.bfloat16
I32 = jnp.int32

UP = [(1, 0), (1, 1)] + [(k, s) for k in (2, 3, 4) for s in (2, 3, 0, 1)]
DN = [(1, 2), (1, 3)] + [(k, s) for k in (2, 3, 4) for s in (0, 1, 2, 3)]
OFF = (2, 1, -1, 0)


def kernel(
    brow, bcol, bdst, weight, m1_in, m2_in, tokens, upstream,
    new_w, new_1, new_2, hidden, in_grad,
    x_all, w_all, w_far, meta, d_all, d_turn, mom1, mom2, seg_b, seg_f, tab_v, tab,
    g_out, g_in, g_own, recv1, q_sum, recv2, zsend, zrecv,
    lsem, ssem, rsem,
):
    dp = lax.axis_index("dp")
    z = lax.axis_index("mp")
    c = lax.rem(dp, 2)
    y = lax.rem(dp // 2, 4)
    x = dp // 8

    def dev(xx, yy, cc, zz):
        return {"dp": (xx * 4 + yy) * 2 + cc, "mp": zz}

    def m4(v):
        return lax.rem(v + 8, 4)

    def m8(v):
        return lax.rem(v + 16, 8)

    zup, zdn = dev(x, y, c, m8(z + 1)), dev(x, y, c, m8(z - 1))
    partner = dev(x, y, 1 - c, z)
    left = {"dp": lax.rem(dp + 31, 32), "mp": z}
    right = {"dp": lax.rem(dp + 1, 32), "mp": z}
    x2, y2 = dev(m4(x + 2), y, c, z), dev(x, m4(y + 2), c, z)
    xp, xm = dev(m4(x + 1), y, c, z), dev(m4(x - 1), y, c, z)
    yp, ym = dev(x, m4(y + 1), c, z), dev(x, m4(y - 1), c, z)

    def plus(h):
        return xp if h == 0 else yp

    def minus(h):
        return xm if h == 0 else ym

    counter = [0]
    pending = []

    def send(src, dst, device):
        i = counter[0]
        counter[0] += 1
        cp = pltpu.make_async_remote_copy(
            src_ref=src, dst_ref=dst, send_sem=ssem.at[i], recv_sem=rsem.at[i],
            device_id=device, device_id_type=MESH,
        )
        cp.start()
        pending.append(cp)
        return i, device

    def arrive(tag, region):
        i, device = tag
        pltpu.make_async_remote_copy(
            src_ref=region, dst_ref=region, send_sem=ssem.at[i], recv_sem=rsem.at[i],
            device_id=device, device_id_type=MESH,
        ).wait_recv()

    lcount = [0]

    def local(src, dst):
        i = lcount[0]
        lcount[0] += 1
        cp = pltpu.make_async_copy(src, dst, lsem.at[i])
        cp.start()
        return cp

    off = {"dp": lax.rem(dp + 31 + 2 * c, 32), "mp": z}
    barrier = pltpu.get_barrier_semaphore()
    for peer in (zup, zdn, partner, off, xp, xm, yp, ym, x2, y2):
        pl.semaphore_signal(barrier, inc=1, device_id=peer, device_id_type=MESH)

    tok_cp = [local(tokens.at[:, pl.ds(i * BS, BS)], x_all.at[z * 8 + i]) for i in range(8)]
    w_cp = local(weight, w_all.at[pl.ds(dp * 4, 4)])
    d_cp = [local(upstream.at[:, pl.ds(i * BS, BS)], d_all.at[i]) for i in range(28)]
    mom_cp = [local(m1_in, mom1.at[1]), local(m2_in, mom2.at[1])]

    sub8 = lax.broadcasted_iota(I32, (8, BS), 0)
    lane8 = lax.broadcasted_iota(I32, (8, BS), 1)
    own_meta = jnp.zeros((8, BS), I32)
    for j in range(4):
        at = lane8 == dp * 4 + j
        for r, ref in enumerate((brow, bcol, bdst)):
            own_meta = own_meta + jnp.where(at & (sub8 == r), ref[j], 0)
    meta[x, y, c] = own_meta

    pl.semaphore_wait(barrier, 10)

    zt = {0: {}, 1: {}}

    def xs(level, s):
        return x_all.at[pl.ds(level * 8 + s * 2, 2)]

    def z_part(dirn, i):
        return i // 4, (i + 2 * dirn) % 4

    def z_send(dirn, i):
        k, s = z_part(dirn, i)
        r = xs(m8(z - k) if dirn == 0 else m8(z + k), s)
        zt[dirn][i] = send(r, r, zup if dirn == 0 else zdn)

    def z_wait(dirn, i):
        k, s = z_part(dirn, i)
        arrive(zt[dirn][i], xs(m8(z - k - 1) if dirn == 0 else m8(z + k + 1), s))

    def z_event(i):
        for dirn in (0, 1):
            z_wait(dirn, i)
            if i + 4 < 14:
                z_send(dirn, i + 4)

    def wp(h, du, dv, cc, j=None):
        xx, yy = (m4(x + du), m4(y + dv)) if h == 0 else (m4(x + dv), m4(y + du))
        base = ((xx * 4 + yy) * 2 + cc) * 4 + h * 2
        return w_all.at[pl.ds(base, 2)] if j is None else w_all.at[pl.ds(base + j, 1)]

    def wf(h, du, cc, j=None):
        base = ((h * 4 + (m4(x + du) if h == 0 else m4(y + du))) * 2 + cc) * 2
        return w_far.at[pl.ds(base, 2)] if j is None else w_far.at[pl.ds(base + j, 1)]

    wt = {}

    def w_send(key, r, device):
        wt[key] = send(r, r, device)

    def w_partner(h, du, dv):
        w_send(("p", h, du, dv), wp(h, du, dv, c), partner)

    def w_phase2(h, du):
        r = wp(h, du, 0, c)
        w_send((2, h, du, 0), r, plus(1 - h))
        w_send((2, h, du, 1), r, minus(1 - h))
        w_partner(h, du, 0)

    def w_turn(h, du):
        arrive(wt[2, h, du, 0], wp(h, du, -1, c))
        wt[3, h, du, 0] = send(wp(h, du, -1, c, 0), wf(h, du, c, 0), plus(1 - h))
        arrive(wt[2, h, du, 1], wp(h, du, 1, c))
        wt[3, h, du, 1] = send(wp(h, du, 1, c, 1), wf(h, du, c, 1), minus(1 - h))
        w_partner(h, du, -1)
        w_partner(h, du, 1)

    def w_last(h, du):
        arrive(wt[3, h, du, 0], wf(h, du, c, 0))
        arrive(wt[3, h, du, 1], wf(h, du, c, 1))
        w_send(("p", h, du, 2), wf(h, du, c), partner)

    for cp in tok_cp:
        cp.wait()
    for i in range(4):
        z_send(0, i)
        z_send(1, i)
    mt = [send(meta.at[x, y, c], meta.at[x, y, c], d) for d in (xp, xm, x2)]
    w_cp.wait()
    for h in (0, 1):
        w_send((0, h, 0), wp(h, 0, 0, c), plus(h))
        w_send((0, h, 1), wp(h, 0, 0, c), minus(h))
    for h in (0, 1):
        w_phase2(h, 0)

    for cp in d_cp:
        cp.wait()
    for i in range(28):
        d_turn[i] = d_all[i].T

    for tag, delta in zip(mt, (-1, 1, 2)):
        arrive(tag, meta.at[m4(x + delta), y, c])
    mt = [send(meta.at[:, y, c], meta.at[:, y, c], d) for d in (yp, ym, y2)]
    z_event(0)
    for h in (0, 1):
        arrive(wt[0, h, 0], wp(h, -1, 0, c))
        w_send((1, h, 0), wp(h, -1, 0, c, 0), plus(h))
        arrive(wt[0, h, 1], wp(h, 1, 0, c))
        w_send((1, h, 1), wp(h, 1, 0, c, 1), minus(h))
    for h in (0, 1):
        w_phase2(h, -1)
        w_phase2(h, 1)
    z_event(1)
    z_event(2)
    for h in (0, 1):
        w_turn(h, 0)
    z_event(3)
    for tag, delta in zip(mt, (-1, 1, 2)):
        arrive(tag, meta.at[:, m4(y + delta), c])
    mt = send(meta.at[:, :, c], meta.at[:, :, c], partner)
    for h in (0, 1):
        arrive(wt[1, h, 0], wp(h, -2, 0, c, 0))
        arrive(wt[1, h, 1], wp(h, 2, 0, c, 1))
        w_phase2(h, 2)
    z_event(4)
    arrive(mt, meta.at[:, :, 1 - c])

    info = jnp.zeros((8, BS), I32)
    for a in range(4):
        for b in range(4):
            for cc in range(2):
                info = info + meta[a, b, cc]
    info = info.astype(F32)
    sub = lax.broadcasted_iota(I32, (BS, BS), 0)
    lane = lax.broadcasted_iota(I32, (BS, BS), 1)
    subf = sub.astype(F32)
    lanef = lane.astype(F32)

    def upright(v):
        return jnp.sum(
            jnp.where(sub == lane, jnp.broadcast_to(v, (BS, BS)), 0.0), axis=1, keepdims=True
        )

    def total(v):
        return jnp.sum(v, axis=0, keepdims=True)

    def ones(mask):
        return jnp.where(mask, 1.0, 0.0)

    row, col, dst = info[0:1], info[1:2], info[2:3]
    row_t, col_t, dst_t = upright(row), upright(col), upright(dst)

    def order(major, minor, major_t, minor_t, span, name_t):
        key, key_t = major * span + minor, major_t * span + minor_t
        pos_t = jnp.sum(ones(key < key_t), axis=1, keepdims=True)
        hot = ones(pos_t == lanef)
        who = total(name_t * hot)
        major_s = total(major_t * hot)
        minor_s = total(minor_t * hot)
        start = total(ones(major_t < major_s))
        keep = jnp.where(start == lanef[0:1], 0.0, 1.0)
        upto = total(ones(major_t <= lanef))
        has = upto - total(ones(major_t < lanef))
        return who, minor_s, keep, jnp.maximum(upto - 1.0, 0.0), jnp.minimum(has, 1.0)

    lane1 = lane8[0:1]
    first_half = lax.rem(lane1 // 2, 2) == 0
    far = jnp.where(
        first_half, ones(lax.rem(lane1 // 8, 4) == m4(y + 2)), ones(lane1 // 32 == m4(x + 2))
    )
    major = far * 64.0 + row
    lane_row = jnp.where(first_half, lane1 // 32, 4 + lax.rem(lane1 // 8, 4))
    in_far = lane_row * 4 + lax.rem(lane1 // 4, 2) * 2 + lax.rem(lane1, 2)
    name = jnp.where(far > 0.0, in_far, lane1).astype(F32)
    rows = list(order(major, col, upright(major), col_t, 32.0, upright(name)))
    rows[0] = jnp.where(lane1 < 96, rows[0], jnp.minimum(rows[0], 31.0))
    z_event(5)
    for h in (0, 1):
        w_turn(h, -1)
        w_turn(h, 1)
    rows = list(order(col, row, col_t, row_t, 64.0, subf)) + rows
    z_event(6)
    hot = ones(dst_t == lanef)
    rows += [total(subf * hot), total(row_t * hot), total(col_t * hot), total(hot)]
    top = [127, 63, 1, 127, 1, 127, 27, 1, 127, 1, 127, 63, 27, 1]
    for i, v in enumerate(rows):
        tab_v[i : i + 1, :] = jnp.clip(v.astype(I32), 0, top[i])
    tab_cp = local(tab_v, tab)

    for h in (0, 1):
        w_last(h, 0)
    z_event(7)
    for h in (0, 1):
        w_turn(h, 2)
    z_event(8)
    for h in (0, 1):
        w_last(h, -1)
        w_last(h, 1)
    z_event(9)
    for h in (0, 1):
        w_last(h, 2)
    for h in (0, 1):
        for du in OFF:
            for dv in (0, -1, 1):
                arrive(wt["p", h, du, dv], wp(h, du, dv, 1 - c))
    tab_cp.wait()

    def run(start, stop, step, acc):
        def some(t, acc):
            for i in range(16):
                acc = step(start + t * 16 + i, acc)
            return acc

        return lax.fori_loop(0, (stop - start) // 16, some, acc)

    def bwd(p, acc, blocks=w_all, top=127):
        prod = lax.dot_general(
            blocks[jnp.minimum(tab[5, p], top)], d_turn[tab[6, p]], (((1,), (0,)), ((), ())),
            preferred_element_type=F32,
        )
        acc = acc * tab[7, p].astype(F32) + prod
        seg_b[p] = acc
        return acc

    acc = run(0, 96, bwd, jnp.zeros((BS, BS), F32))
    for h in (0, 1):
        for du in OFF:
            arrive(wt["p", h, du, 2], wf(h, du, 1 - c))
    acc = run(96, 128, lambda p, acc: bwd(p, acc, w_far, 31), acc)

    def own_part(r):
        near = seg_b[tab[8, r]] * (tab[9, r].astype(F32) * SCALE)
        return near + seg_b[tab[8, 64 + r]] * (tab[9, 64 + r].astype(F32) * SCALE)

    zr = {0: {}, 1: {}}

    def zr_send(dirn, i):
        k, s = (UP, DN)[dirn][i]
        level = m8(z + 5 - k) if dirn == 0 else m8(z - 5 + k)
        if i >= 4:
            arrive(zr[dirn][i - 4], zrecv.at[dirn, i - 4])
        for b in range(2):
            v = own_part(level * 8 + s * 2 + b)
            if i >= 4:
                v = v + zrecv[dirn, i - 4, b].astype(F32)
            zsend[dirn, i, b] = v.astype(BF16)
        zr[dirn][i] = send(zsend.at[dirn, i], zrecv.at[dirn, i], zup if dirn == 0 else zdn)

    def zr_event(i):
        zr_send(0, i)
        zr_send(1, i)

    for i in range(4):
        zr_event(i)

    for cp in mom_cp:
        cp.wait()
    mom_t = []
    for ref in (mom1, mom2):
        mom_t.append((send(ref.at[1], ref.at[0], right), ref.at[0]))
        mom_t.append((send(ref.at[1], ref.at[2], left), ref.at[2]))
    for i in range(10, 14):
        z_event(i)

    def grad(g, h, j, o, cc):
        u, v = OFF[g], OFF[o]
        xx, yy = (m4(x + u), m4(y + v)) if h == 0 else (m4(x + v), m4(y + u))
        q = ((xx * 4 + yy) * 2 + cc) * 4 + h * 2 + j
        r = lax.dot_general(
            x_all[tab[11, q]], d_all[tab[12, q]], (((0,), (0,)), ((), ())),
            preferred_element_type=F32,
        )
        return r * (tab[13, q].astype(F32) * SCALE)

    gt = {}
    members = [(j, o) for j in (0, 1) for o in range(4)]
    for g in range(4):
        for h in (0, 1):
            for j, o in members:
                g_out[g, h, j, o] = grad(g, h, j, o, 1 - c).astype(BF16)
            gt[g, h] = send(g_out.at[g, h], g_in.at[g, h], partner)

    def fwd(p, acc):
        prod = jnp.dot(x_all[tab[1, p]], w_all[tab[0, p]], preferred_element_type=F32)
        acc = acc * tab[2, p].astype(F32) + prod
        seg_f[p] = acc
        return acc

    zr_event(4)
    for h in (0, 1):
        for a in range(4):
            xx, yy = (a, m4(y + 2)) if h == 0 else (m4(x + 2), a)
            for cc in (0, 1):
                for j in (0, 1):
                    w_all[((xx * 4 + yy) * 2 + cc) * 4 + h * 2 + j] = w_far[((h * 4 + a) * 2 + cc) * 2 + j]
    facc = run(0, 32, fwd, jnp.zeros((BS, BS), F32))

    rt = {}

    def halves(ref, u):
        return ref.at[pl.ds(2 * u, 2)]

    def g1_send(h, dirn, n, u, g, j):
        rt[h, dirn, n, u] = send(
            g_own.at[g, h, j, pl.ds(2 * u, 2)], recv1.at[h, dirn, n, pl.ds(2 * u, 2)],
            plus(h) if dirn == 0 else minus(h),
        )

    def g1_direct(h, dirn, u):
        g1_send(h, dirn, 1, u, 1 + dirn, 1 - dirn)

    def g1_arrive(h, dirn, n, u):
        arrive(rt[h, dirn, n, u], recv1.at[h, dirn, n, pl.ds(2 * u, 2)])

    def own_group(g):
        for h in (0, 1):
            arrive(gt[g, h], g_in.at[g, h])
            for j, o in members:
                v = grad(g, h, j, o, c) + g_in[g, h, j, o].astype(F32)
                g_own[g, h, j, o] = v.astype(BF16)
            if g == 0:
                for u in (0, 1):
                    g1_send(h, 0, 0, u, 0, 0)
                    g1_send(h, 1, 0, u, 0, 1)
            elif g < 3:
                g1_direct(h, g - 1, 0)

    def g1_step(u):
        for h in (0, 1):
            for dirn in (0, 1):
                g1_arrive(h, dirn, 0, u)
                g, j = (1, 0) if dirn == 0 else (2, 1)
                for o in (2 * u, 2 * u + 1):
                    v = g_own[g, h, j, o].astype(F32) + recv1[h, dirn, 0, o].astype(F32)
                    g_own[g, h, j, o] = v.astype(BF16)
                g1_send(h, dirn, 2, u, g, j)
                if u == 0:
                    g1_direct(h, dirn, 1)

    st = {}

    def g2_send(h, dirn, n, j, o):
        st[h, dirn, n] = send(
            q_sum.at[h, j, o], recv2.at[h, dirn, n], plus(1 - h) if dirn == 0 else minus(1 - h)
        )

    def g1_end(u):
        for h in (0, 1):
            for dirn in (0, 1):
                g1_arrive(h, dirn, 1, u)
                g1_arrive(h, dirn, 2, u)
            for j in (0, 1):
                lo, hi = (2, 1) if j == 0 else (1, 2)
                for o in (2 * u, 2 * u + 1):
                    v = (
                        g_own[3, h, j, o].astype(F32)
                        + recv1[h, 0, lo, o].astype(F32)
                        + recv1[h, 1, hi, o].astype(F32)
                    )
                    q_sum[h, j, o] = v.astype(BF16)
            if u == 0:
                g2_send(h, 0, 0, 0, 0)
                g2_send(h, 1, 0, 1, 0)
                g2_send(h, 0, 1, 1, 1)
            else:
                g2_send(h, 1, 1, 0, 2)

    def drain(count):
        for cp in pending[:count]:
            cp.wait_send()
        del pending[:count]

    own_group(0)
    zr_event(5)
    own_group(1)
    own_group(2)
    zr_event(6)
    own_group(3)
    facc = run(32, 48, fwd, facc)
    zr_event(7)
    facc = run(48, 64, fwd, facc)
    zr_event(8)
    g1_step(0)
    facc = run(64, 80, fwd, facc)
    zr_event(9)
    g1_step(1)
    facc = run(80, 96, fwd, facc)
    zr_event(10)
    facc = run(96, 128, fwd, facc)
    zr_event(11)
    for i in range(28):
        v = seg_f[tab[3, i]] * (tab[4, i].astype(F32) * SCALE)
        hidden[:, i * BS : (i + 1) * BS] = v.astype(BF16)
    zr_event(12)
    g1_end(0)
    zr_event(13)
    g1_end(1)
    drain(len(pending) - 40)

    def in_part(s):
        iu, id_ = UP.index((4, s)), DN.index((4, s))
        for k in range(2):
            b = s * 2 + k
            v = own_part(z * 8 + b) + zrecv[0, iu, k].astype(F32) + zrecv[1, id_, k].astype(F32)
            in_grad[:, b * BS : (b + 1) * BS] = v.T.astype(BF16)

    def z_last(i):
        for dirn in (0, 1):
            arrive(zr[dirn][i], zrecv.at[dirn, i])

    z_last(10)
    for h in (0, 1):
        for dirn in (0, 1):
            arrive(st[h, dirn, 0], recv2.at[h, dirn, 0])
            at = (h, 0, 1) if dirn == 0 else (h, 1, 2)
            q_sum[at] = (q_sum[at].astype(F32) + recv2[h, dirn, 0].astype(F32)).astype(BF16)
            g2_send(h, dirn, 2, at[1], at[2])
    for tag, region in mom_t:
        arrive(tag, region)
    z_last(11)
    drain(len(pending) - 12)
    z_last(12)
    in_part(0)
    in_part(2)
    z_last(13)
    in_part(1)
    in_part(3)

    for h in (0, 1):
        for dirn in (0, 1):
            arrive(st[h, dirn, 1], recv2.at[h, dirn, 1])
            arrive(st[h, dirn, 2], recv2.at[h, dirn, 2])
        for j in (0, 1):
            lo, hi = (2, 1) if j == 0 else (1, 2)
            g = (
                q_sum[h, j, 3].astype(F32)
                + recv2[h, 0, lo].astype(F32)
                + recv2[h, 1, hi].astype(F32)
            )
            q = dp * 4 + h * 2 + j
            s = tab[10, q]
            valid = tab[13, q].astype(F32)
            mi = jnp.clip(s - (dp - 1) * 4, 0, 11)
            first = B1 * mom1[mi // 4, lax.rem(mi, 4)] + (1.0 - B1) * g
            second = B2 * mom2[mi // 4, lax.rem(mi, 4)] + (1.0 - B2) * g * g
            stepped = w_all[s].astype(F32) - LEARN * first / (jnp.sqrt(second) + EPS)
            new_w[h * 2 + j] = (stepped * valid).astype(BF16)
            new_1[h * 2 + j] = first * valid
            new_2[h * 2 + j] = second * valid

    for cp in pending:
        cp.wait_send()


def store(a, b, c, d, e, oa, ob, oc, od, oe, sem):
    copies = [
        pltpu.make_async_copy(src, dst, sem.at[i])
        for i, (src, dst) in enumerate(((a, oa), (b, ob), (c, oc), (d, od), (e, oe)))
    ]
    for cp in copies:
        cp.start()
    for cp in copies:
        cp.wait()


def body(weight, moment_one, moment_two, block_row, block_col, dest_slot, tokens, upstream):
    hbm = pl.BlockSpec(memory_space=pl.ANY)
    smem = pl.BlockSpec(memory_space=pltpu.SMEM)
    vmem = pl.BlockSpec(memory_space=pltpu.VMEM)
    outs = (
        ((4, BS, BS), BF16), ((4, BS, BS), F32), ((4, BS, BS), F32),
        ((128, 3584), BF16), ((128, 1024), BF16),
    )
    made = pl.pallas_call(
        kernel,
        name="step",
        out_shape=tuple(pltpu.VMEM(s, t) for s, t in outs),
        in_specs=[smem] * 3 + [hbm] * 5,
        out_specs=(vmem,) * 5,
        scratch_shapes=[
            pltpu.VMEM((64, BS, BS), BF16),
            pltpu.VMEM((BS, BS, BS), BF16),
            pltpu.VMEM((32, BS, BS), BF16),
            pltpu.VMEM((4, 4, 2, 8, BS), I32),
            pltpu.VMEM((28, BS, BS), BF16),
            pltpu.VMEM((28, BS, BS), BF16),
            pltpu.VMEM((3, 4, BS, BS), F32),
            pltpu.VMEM((3, 4, BS, BS), F32),
            pltpu.VMEM((BS, BS, BS), F32),
            pltpu.VMEM((BS, BS, BS), F32),
            pltpu.VMEM((16, BS), I32),
            pltpu.SMEM((16, BS), I32),
            pltpu.VMEM((4, 2, 2, 4, BS, BS), BF16),
            pltpu.VMEM((4, 2, 2, 4, BS, BS), BF16),
            pltpu.VMEM((4, 2, 2, 4, BS, BS), BF16),
            pltpu.VMEM((2, 2, 3, 4, BS, BS), BF16),
            pltpu.VMEM((2, 2, 4, BS, BS), BF16),
            pltpu.VMEM((2, 2, 3, BS, BS), BF16),
            pltpu.VMEM((2, 14, 2, BS, BS), BF16),
            pltpu.VMEM((2, 14, 2, BS, BS), BF16),
            pltpu.SemaphoreType.DMA((48,)),
            pltpu.SemaphoreType.DMA((NSEM,)),
            pltpu.SemaphoreType.DMA((NSEM,)),
        ],
        compiler_params=pltpu.CompilerParams(
            collective_id=0, has_side_effects=True, vmem_limit_bytes=62 * 1024 * 1024
        ),
    )(block_row, block_col, dest_slot, weight, moment_one, moment_two, tokens, upstream)
    return pl.pallas_call(
        store,
        name="store",
        out_shape=tuple(jax.ShapeDtypeStruct(s, t) for s, t in outs),
        in_specs=[pl.BlockSpec(memory_space=pltpu.VMEM)] * 5,
        out_specs=(hbm,) * 5,
        scratch_shapes=[pltpu.SemaphoreType.DMA((5,))],
        compiler_params=pltpu.CompilerParams(vmem_limit_bytes=2 * 1024 * 1024),
    )(*made)


def solution(mesh):
    return jax.shard_map(
        body,
        mesh=mesh,
        in_specs=(
            P(("dp", "mp"), None, None),
            P(("dp", "mp"), None, None),
            P(("dp", "mp"), None, None),
            P(("dp", "mp")),
            P(("dp", "mp")),
            P(("dp", "mp")),
            P("dp", "mp"),
            P("dp", "mp"),
        ),
        out_specs=(
            P(("dp", "mp"), None, None),
            P(("dp", "mp"), None, None),
            P(("dp", "mp"), None, None),
            P("dp", "mp"),
            P("dp", "mp"),
        ),
        check_vma=False,
    )
```
